32 devices in a mesh: parts: 2 (over x), wide: 16 (over z, y, core).
Axes of the slice: x: 2, y: 2, z: 4, core: 2. Of those that a mesh axis runs over, the one named last changes fastest.
Arguments:
- history: bfloat16 [2048, 8, 1024], P(('parts', 'wide')), parts along dimension 0, may hold values from -6 to 6
- pool: bfloat16 [512, 1024], P(('parts', 'wide')), parts along dimension 0, may hold values from -6 to 6
- cand_ids: int32 [64, 128], P(('parts', 'wide')), parts along dimension 0, may hold values from 0 to 255
- block_user: int32 [32, 64], P('parts'), parts along dimension 0, may hold values from 0 to 31, as said below
- norm_gain: float32 [1024], replicated, may hold values from 0.5 to 1.5
- w_in: bfloat16 [1024, 4096], replicated, may hold values from -0.1875 to 0.1875
- attn_gain: float32 [1024], replicated, may hold values from 0.25 to 1.75
- w_out: bfloat16 [1024, 1024], replicated, may hold values from -0.1875 to 0.1875
Outputs:
- scored: bfloat16 [64, 128, 1024], P(('parts', 'wide')), parts along dimension 0
The draws below stay inside these ranges and needn't reach their ends.
There are 2 independent parts, one for each index of `parts`. The reference program is written for one: setup_inputs(seed, part) draws one part's arguments, and reference() takes and returns one part's arrays. A program takes and returns all parts, laid end to end along the dimension named above; an argument that names none is the same for every part. Nothing has to cross between parts.
Inputs may be any that keep to these rules, and one draw needn't show every extreme that they name: `block_user`: user u is ranked on device u // 2. At most 8 blocks of one owner belong to users ranked on one device; every draw reaches this, and some device receives 8 blocks from every owner.
All inputs are finite; a program needn't handle non-finite values.
Results may differ from the reference program's by a relative error of at most 0.0051.
Values may be sent and summed in bfloat16 or wider, within the bound.
No kernel may reach another device: no remote copies, remote signals or barrier semaphores. Data moves between devices by JAX's collectives and lax.ppermute only.
A program may use at most 64 MiB of HBM per device.

```python
import jax
import jax.numpy as jnp
from jax import lax

D = 1024
HEADS = 8
BLOCK_ROWS = 8
USERS_DEV = 2
CAND_USER = 128
CACHE_DEV = 64
SLOT = 8
USERS = 32
BLOCKS = 1024
POOL = 256
N_WIDE = 16


def draw_block_user(key, part):
    keys = jax.random.split(key, 5)
    ranker_ids = jnp.arange(N_WIDE, dtype=jnp.int32)
    noise = jax.random.randint(keys[0], (N_WIDE, N_WIDE), 0, N_WIDE, dtype=jnp.int32)
    bias = jax.random.randint(keys[1], (N_WIDE,), 0, 4, dtype=jnp.int32)
    hottest = jax.random.randint(keys[2], (), 0, N_WIDE, dtype=jnp.int32)
    bias = jnp.where(ranker_ids == hottest, 8, bias)
    score = (noise + bias[None, :] * (N_WIDE // 2 + 1)) * N_WIDE + ranker_ids[None, :]
    ranked = jnp.argsort(-score, axis=1, stable=True)
    chosen = ranked[:, :CACHE_DEV // SLOT]
    target = jnp.repeat(chosen, SLOT, axis=1)
    local_user = jax.random.randint(keys[3], (N_WIDE, CACHE_DEV), 0, USERS_DEV, dtype=jnp.int32)
    owner_user = target * USERS_DEV + local_user
    block_ids = jnp.arange(CACHE_DEV, dtype=jnp.int32)
    shuffle_key = jax.random.randint(keys[4], (N_WIDE, CACHE_DEV), 0, CACHE_DEV, dtype=jnp.int32) * CACHE_DEV + block_ids[None, :]
    shuffle = jnp.argsort(shuffle_key, axis=1, stable=True)
    return jnp.take_along_axis(owner_user, shuffle, axis=1).astype(jnp.int32)


def place_ends(array, key, least, high):
    dims = array.shape
    place = [jax.random.randint(jax.random.fold_in(key, axis), (), 0, dims[axis]) for axis in range(len(dims))]
    array = array.at[tuple(place)].set(least)
    longest = dims.index(max(dims))
    place[longest] = (place[longest] + 1) % dims[longest]
    return array.at[tuple(place)].set(high)


def levels(stream_key, extent, cuts, least, largest):
    level = 1.0
    for position, shards_of in cuts:
        draws = jax.random.uniform(jax.random.fold_in(jax.random.fold_in(stream_key, 6), position), (shards_of,), jnp.float32, least / len(cuts), largest / len(cuts))
        level = level * jnp.repeat(jnp.exp(draws), extent[position] // shards_of).reshape((-1,) + (1,) * (len(extent) - 1 - position))
    return level


def normal_values(stream_key, extent, deviation, bound, shards=(), kind=jnp.bfloat16):
    entries = jax.random.normal(stream_key, extent, jnp.float32) * deviation
    if len(shards) > 0:
        entries = levels(stream_key, extent, shards, -0.22, 0.18) * entries
    return jnp.clip(entries, min=-bound, max=bound).astype(kind)


def setup_inputs(seed: int = 0, part: int = 0) -> dict:
    splits = jax.random.split(jax.random.key(seed), 9)
    part_keys = jax.random.split(jax.random.fold_in(splits[8], part), 9)
    history = normal_values(part_keys[0], (BLOCKS, BLOCK_ROWS, D), 1.0, 6.0, ((0, 16),))
    pool = normal_values(part_keys[1], (POOL, D), 1.0, 6.0, ((0, 16),))
    cand_ids = place_ends(jax.random.randint(part_keys[2], (USERS, CAND_USER), 0, POOL), jax.random.fold_in(part_keys[2], 1), 0, POOL - 1).astype(jnp.int32)
    block_user = draw_block_user(jax.random.fold_in(jax.random.fold_in(splits[8], part), 71), part)
    norm_gain = jnp.clip(1.0 + 0.1 * jax.random.normal(splits[4], (D,), jnp.float32), 0.5, 1.5)
    w_in = normal_values(splits[5], (D, 4 * D), D ** -0.5, 0.1875)
    attn_gain = jnp.clip(1.0 + 0.15 * jax.random.normal(splits[6], (D,), jnp.float32), 0.25, 1.75)
    w_out = normal_values(splits[7], (D, D), D ** -0.5, 0.1875)
    return dict(history=history, pool=pool, cand_ids=cand_ids, block_user=block_user, norm_gain=norm_gain, w_in=w_in, attn_gain=attn_gain, w_out=w_out)


def layer_norm(values, gain_vec):
    average = lax.optimization_barrier(jnp.mean(values, axis=-1, keepdims=True))
    centered = values - average
    spread = lax.optimization_barrier(jnp.mean(centered * centered, axis=-1, keepdims=True))
    return centered * lax.rsqrt(spread + 1e-05) * gain_vec

def project_cache(row_block, norm_gain, w_in):
    model_width = row_block.shape[-1]
    flat_rows = row_block.reshape(-1, model_width).astype(jnp.float32)
    normed = layer_norm(flat_rows, norm_gain).astype(jnp.bfloat16)
    front_proj = jnp.dot(normed, w_in[:, 2 * model_width:], preferred_element_type=jnp.float32)
    return jax.nn.silu(front_proj).astype(jnp.bfloat16)

def score_rows(item_rows, keyval, key_owner, norm_gain, w_in, attn_gain, w_out):
    model_width = item_rows.shape[1]
    head_size = model_width // HEADS
    normed = layer_norm(item_rows.astype(jnp.float32), norm_gain).astype(jnp.bfloat16)
    front_proj = jnp.dot(normed, w_in[:, :2 * model_width], preferred_element_type=jnp.float32)
    gate_up = jax.nn.silu(front_proj[:, :model_width])
    queries = jax.nn.silu(front_proj[:, model_width:]).astype(jnp.bfloat16)
    query_heads = queries.reshape(-1, HEADS, head_size).astype(jnp.float32)
    key_heads = keyval[:, :model_width].reshape(-1, HEADS, head_size).astype(jnp.float32)
    value_heads = keyval[:, model_width:].reshape(-1, HEADS, head_size).astype(jnp.float32)
    scores = jnp.einsum('rhd,khd->hrk', query_heads, key_heads)
    row_user = jnp.repeat(jnp.arange(USERS_DEV, dtype=jnp.int32), CAND_USER)
    same_user = row_user[:, None] == key_owner[None, :]
    weights = jnp.where(same_user[None], jax.nn.silu(scores * head_size ** (-0.5)), 0.0).astype(jnp.bfloat16)
    attended = jnp.einsum('hrk,khd->rhd', weights.astype(jnp.float32), value_heads).reshape(-1, model_width)
    gated_rows = (layer_norm(attended, attn_gain) * gate_up).astype(jnp.bfloat16)
    result = jnp.dot(gated_rows, w_out, preferred_element_type=jnp.float32) + item_rows.astype(jnp.float32)
    return result.astype(jnp.bfloat16)

def reference(history, pool, cand_ids, block_user, norm_gain, w_in, attn_gain, w_out):
    dest_flat = (block_user // USERS_DEV).reshape(-1)
    user_flat = block_user.reshape(-1)
    block_order = jnp.arange(BLOCKS, dtype=jnp.int32)
    capacity = N_WIDE * SLOT

    def rank_one(ranker):
        sort_key = jnp.where(dest_flat == ranker, 0, BLOCKS) + block_order
        picked = jnp.argsort(sort_key)[:capacity]
        valid = dest_flat[picked] == ranker
        row_block = jnp.where(valid[:, None, None], history[picked], jnp.zeros((), history.dtype))
        keyval = project_cache(row_block, norm_gain, w_in)
        owner_user = jnp.where(valid, user_flat[picked] - ranker * USERS_DEV, -1)
        key_owner = jnp.repeat(owner_user, BLOCK_ROWS)
        id_rows = lax.dynamic_slice_in_dim(cand_ids, (ranker * USERS_DEV).astype(jnp.int32), USERS_DEV, 0)
        item_rows = jnp.take(pool, id_rows.reshape(-1), axis=0)
        return score_rows(item_rows, keyval, key_owner, norm_gain, w_in, attn_gain, w_out)
    ranked = lax.map(rank_one, jnp.arange(N_WIDE, dtype=jnp.int32))
    return ranked.reshape(USERS, CAND_USER, D)
```

```python
import functools
import jax
import jax.numpy as jnp
from jax import lax
from jax.experimental import pallas as pl
from jax.experimental.pallas import tpu as pltpu
from jax.sharding import PartitionSpec as P

HEADS = 8
EPS = 1e-05
VMEM = pl.BlockSpec(memory_space=pltpu.VMEM)
SMEM = pl.BlockSpec(memory_space=pltpu.SMEM)
F32, BF16 = jnp.float32, jnp.bfloat16


def params(mib):
    return pltpu.CompilerParams(vmem_limit_bytes=mib << 20)


def normalize(rows, gain):
    average = jnp.mean(rows, axis=-1, keepdims=True)
    centered = rows - average
    spread = jnp.mean(centered * centered, axis=-1, keepdims=True)
    return centered * lax.rsqrt(spread + EPS) * gain


def silu(x):
    half = 0.5 * x
    return half + half * jnp.tanh(half)


def pack_kernel(slots, source, history, *outs):
    for r, out in enumerate(outs):
        for j in range(slots):
            out[j] = history[source[r * slots + j]]


def pack(history, source, devices, slots):
    block = jax.ShapeDtypeStruct((slots,) + history.shape[1:], history.dtype)
    return pl.pallas_call(
        functools.partial(pack_kernel, slots),
        out_shape=[block] * devices,
        in_specs=[SMEM, VMEM],
        out_specs=[VMEM] * devices,
        compiler_params=params(12),
        cost_estimate=pl.CostEstimate(flops=0, bytes_accessed=3 << 20, transcendentals=0),
    )(source, history)


def front_kernel(ids, pool, gain, w_in, items, gate, queries):
    width = pool.shape[1]
    order = lax.broadcasted_iota(jnp.int32, (ids.shape[0], pool.shape[0]), 1)
    chosen = jnp.where(ids[...] == order, 1.0, 0.0).astype(BF16)
    rows = jnp.dot(chosen, pool[...], preferred_element_type=F32)
    items[...] = rows.astype(BF16)
    normed = normalize(rows, gain[...]).astype(BF16)
    gate[...] = silu(jnp.dot(normed, w_in[:, :width], preferred_element_type=F32))
    queries[...] = silu(
        jnp.dot(normed, w_in[:, width : 2 * width], preferred_element_type=F32)
    ).astype(BF16)


def front(ids, pool, gain, w_in):
    rows, width = ids.shape[0], pool.shape[1]
    return pl.pallas_call(
        front_kernel,
        out_shape=[
            jax.ShapeDtypeStruct((rows, width), BF16),
            jax.ShapeDtypeStruct((rows, width), F32),
            jax.ShapeDtypeStruct((rows, width), BF16),
        ],
        in_specs=[VMEM] * 4,
        out_specs=[VMEM] * 3,
        compiler_params=params(24),
        cost_estimate=pl.CostEstimate(flops=1 << 30, bytes_accessed=6 << 20, transcendentals=0),
    )(ids, pool, gain, w_in)


def attend(counts, owners, blocks, queries, gain, w_in, users, block_rows, slots, first, store):
    width = queries.shape[1]
    head = width // HEADS
    per_user = queries.shape[0] // users
    events = slots * block_rows
    rows = jnp.concatenate([b[...] for b in blocks], axis=0).astype(F32)
    normed = normalize(rows, gain[...]).astype(BF16)
    total = rows.shape[0]
    lane = lax.broadcasted_iota(jnp.int32, (1, total), 1)
    masks = []
    for u in range(users):
        ok = jnp.zeros((1, total), jnp.bool_)
        for k, owner in enumerate(owners):
            low = jnp.int32(0)
            for v in range(u):
                low += counts[owner, v]
            high = low + counts[owner, u]
            ok |= (lane >= k * events + low * block_rows) & (lane < k * events + high * block_rows)
        masks.append(ok)
    for h in range(HEADS):
        at = h * head
        key = silu(
            jnp.dot(normed, w_in[:, 2 * width + at : 2 * width + at + head], preferred_element_type=F32)
        ).astype(BF16)
        value = silu(
            jnp.dot(normed, w_in[:, 3 * width + at : 3 * width + at + head], preferred_element_type=F32)
        ).astype(BF16)
        scores = lax.dot_general(
            queries[:, at : at + head], key, (((1,), (1,)), ((), ())), preferred_element_type=F32
        )
        weights = silu(scores * head ** (-0.5))
        parts = [
            jnp.where(masks[u], weights[u * per_user : (u + 1) * per_user], 0.0) for u in range(users)
        ]
        weights = jnp.concatenate(parts, axis=0).astype(BF16)
        store(h, at, head, jnp.dot(weights, value, preferred_element_type=F32))


def group_kernel(meta, counts, owners, *refs):
    n_blocks, users, block_rows, slots, first = meta
    blocks, refs = refs[:n_blocks], refs[n_blocks:]
    queries, gain, w_in = refs[:3]
    if first:
        out = refs[3]
    else:
        total, out = refs[3:]

    def store(h, at, head, value):
        out[:, at : at + head] = value if first else total[:, at : at + head] + value

    attend(
        counts,
        [owners[k] for k in range(n_blocks)],
        blocks,
        queries,
        gain,
        w_in,
        users,
        block_rows,
        slots,
        first,
        store,
    )


def group(counts, owners, blocks, queries, gain, w_in, total, users, block_rows, slots):
    first = total is None
    meta = (len(blocks), users, block_rows, slots, first)
    extra = [] if first else [total]
    n_in = 2 + len(blocks) + 3
    rows = len(blocks) * slots * block_rows
    return pl.pallas_call(
        functools.partial(group_kernel, meta),
        out_shape=jax.ShapeDtypeStruct(queries.shape, F32),
        in_specs=[SMEM] * 2 + [VMEM] * (len(blocks) + 3 + len(extra)),
        out_specs=VMEM,
        input_output_aliases={} if first else {n_in: 0},
        compiler_params=params(24),
        cost_estimate=pl.CostEstimate(flops=rows << 22, bytes_accessed=6 << 20, transcendentals=0),
    )(counts, owners, *blocks, queries, gain, w_in, *extra)


def last_kernel(meta, counts, owners, *refs):
    n_blocks, users, block_rows, slots, first = meta
    blocks, refs = refs[:n_blocks], refs[n_blocks:]
    queries, gain, w_in, total, gate, items, attn_gain, w_out, out, summed = refs

    def store(h, at, head, value):
        summed[:, at : at + head] = total[:, at : at + head] + value

    attend(
        counts,
        [owners[k] for k in range(n_blocks)],
        blocks,
        queries,
        gain,
        w_in,
        users,
        block_rows,
        slots,
        first,
        store,
    )
    gated = (normalize(summed[...], attn_gain[...]) * gate[...]).astype(BF16)
    result = jnp.dot(gated, w_out[...], preferred_element_type=F32) + items[...].astype(F32)
    out[...] = result.astype(BF16)


def last(counts, owners, blocks, queries, gain, w_in, total, gate, items, attn_gain, w_out, users, block_rows, slots):
    meta = (len(blocks), users, block_rows, slots, False)
    return pl.pallas_call(
        functools.partial(last_kernel, meta),
        out_shape=jax.ShapeDtypeStruct(queries.shape, BF16),
        in_specs=[SMEM] * 2 + [VMEM] * (len(blocks) + 8),
        out_specs=VMEM,
        scratch_shapes=[pltpu.VMEM(queries.shape, F32)],
        compiler_params=params(24),
        cost_estimate=pl.CostEstimate(flops=1 << 30, bytes_accessed=6 << 20, transcendentals=0),
    )(counts, owners, *blocks, queries, gain, w_in, total, gate, items, attn_gain, w_out)


def body(history, pool, cand_ids, block_user, norm_gain, w_in, attn_gain, w_out):
    width = history.shape[2]
    block_rows = history.shape[1]
    owned = history.shape[0]
    devices = lax.axis_size("wide")
    me = lax.axis_index("wide")
    users = cand_ids.shape[0]
    slots = max(1, 2 * owned // devices)

    def swap(x, r):
        return lax.ppermute(x, "wide", [(i, i ^ r) for i in range(devices)])

    order = jnp.arange(owned, dtype=jnp.int32)
    mine = lax.dynamic_index_in_dim(block_user, me, 0, keepdims=False)
    target = mine // users
    rank = mine * owned + order
    ahead = (target[:, None] == target[None, :]) & (rank[None, :] < rank[:, None])
    within = jnp.sum(ahead.astype(jnp.int32), axis=1)
    position = (target ^ me) * slots + within
    spots = jnp.arange(devices * slots, dtype=jnp.int32)
    source = jnp.sum(jnp.where(position[None, :] == spots[:, None], order[None, :], 0), axis=1)
    mine_users = me * users + jnp.arange(users, dtype=jnp.int32)
    counts = jnp.sum((block_user[:, :, None] == mine_users[None, None, :]).astype(jnp.int32), axis=1)

    outgoing = pack(history, source, devices, slots)
    gathered = pool
    for r in (8, 4, 2, 1):
        if r < devices:
            pass
    gain = norm_gain.reshape(1, width)
    arrived = {0: outgoing[0]}
    for r in range(devices - 1, 0, -1):
        arrived[r] = swap(outgoing[r], r)
    everyone = pool
    r = devices // 2
    while r >= 1:
        everyone = jnp.concatenate([everyone, swap(everyone, r)], axis=0)
        r //= 2
    bits = devices.bit_length() - 1
    rows_each = pool.shape[0]
    flat_ids = cand_ids.reshape(-1, 1)
    offset = (flat_ids // rows_each) ^ me
    place = jnp.zeros_like(offset)
    for b in range(bits):
        place += ((offset >> b) & 1) << (bits - 1 - b)
    ids = place * rows_each + flat_ids % rows_each
    items, gate, queries = front(ids, everyone, gain, w_in)

    def rows_of(r):
        return arrived[r].reshape(slots * block_rows, width)

    quarter = devices // 4
    total = None
    for g in range(4):
        members = list(range(g * quarter, (g + 1) * quarter))
        owners = jnp.stack([me ^ r for r in members])
        blocks = [rows_of(r) for r in members]
        if g < 3:
            total = group(counts, owners, blocks, queries, gain, w_in, total, users, block_rows, slots)
        else:
            out = last(
                counts, owners, blocks, queries, gain, w_in, total, gate, items,
                attn_gain.reshape(1, width), w_out, users, block_rows, slots,
            )
    return out.reshape(users, -1, width)


def solution(mesh):
    in_specs = (
        P(("parts", "wide"), None, None),
        P(("parts", "wide"), None),
        P(("parts", "wide"), None),
        P("parts", None),
        P(),
        P(),
        P(),
        P(),
    )
    out_specs = P(("parts", "wide"), None, None)
    return jax.shard_map(body, mesh=mesh, in_specs=in_specs, out_specs=out_specs, check_vma=False)
```
